32 devices in a mesh: group: 2 (over y), tensor: 4 (over z), dp: 4 (over x, core).
Axes of the slice: x: 2, y: 2, z: 4, core: 2. Of those that a mesh axis runs over, the one named last changes fastest.
Arguments:
- teacher_input: bfloat16 [16, 257, 6144], P(('group', 'dp')), parts along dimension 0, may hold values from -1000 to 1000
- teacher_gain: float32 [6144], replicated, may hold values from 0.5 to 2
- teacher_weight: bfloat16 [6144, 2, 6144], P('dp', None, 'tensor'), may hold values from -30 to 30
- head_counts: int32 [48, 16], replicated, may hold values from 0 to 3
- assignment: int32 [16], P(('group', 'dp')), parts along dimension 0, may hold values from 0 to 7, each once
- student_input: bfloat16 [16, 257, 1024], P(('group', 'dp')), parts along dimension 0, may hold values from -1000 to 1000
- student_gain: float32 [1024], replicated, may hold values from 0.5 to 2
- student_bias: float32 [1024], replicated, may hold values from -3 to 3
- student_weight: bfloat16 [1024, 2048], P(None, 'tensor'), may hold values from -30 to 30
Outputs:
- weight_grad: float32 [2048, 2048], P('group', 'tensor'), parts along dimension 0
The draws below stay inside these ranges and needn't reach their ends.
There are 2 independent parts, one for each index of `group`. The reference program is written for one: setup_inputs(seed, part) draws one part's arguments, and reference() takes and returns one part's arrays. A program takes and returns all parts, laid end to end along the dimension named above; an argument that names none is the same for every part. Nothing has to cross between parts.
Inputs may be any that keep to these rules, and one draw needn't show every extreme that they name: `assignment`: every image index of the group appears exactly once.
All inputs are finite; a program needn't handle non-finite values.
Results may differ from the reference program's by a relative error of at most 0.013.
The reference program's roundings to bfloat16 on the way count: a program that leaves them out, or rounds other values in their place, can miss the bound.
Values may be sent and summed in bfloat16 or wider, within the bound.
A program may use at most 192 MiB of HBM per device.

```python
import math
import jax
import jax.numpy as jnp
from jax import lax

D_T = 6144
HEADS_T = 48
HD_T = 128
D_S = 1024
HEADS_S = 16
HD_S = 64
TOKENS = 257
QROWS = 128
IMAGES = 8
DIVISOR = 72
N_TENSOR = 4


def rough_input(key, width):
    keys = jax.random.split(key, 4)
    base = jax.random.normal(keys[0], (IMAGES, TOKENS, width), jnp.float32)
    scales = jnp.exp(jax.random.uniform(keys[2], (IMAGES, TOKENS, 1), jnp.float32, 0.0, math.log(10.0)))
    columns = jnp.exp(jax.random.uniform(keys[3], (width,), jnp.float32, 0.0, math.log(10.0)))
    return jnp.clip(base, -6.0, 6.0) * columns * scales


def rough_weight(key, width, heads, size):
    keys = jax.random.split(key, 2)
    query = jnp.clip(jax.random.normal(keys[0], (width, heads, size), jnp.float32), -4.0, 4.0) / math.sqrt(width)
    other = jnp.clip(jax.random.normal(keys[1], (width, heads, size), jnp.float32), -4.0, 4.0) / math.sqrt(width)
    return (query, other)


def draw_teacher_input(key, part):
    return rough_input(key, D_T).astype(jnp.bfloat16)


def draw_student_input(key, part):
    return rough_input(jax.random.fold_in(key, 7), D_S).astype(jnp.bfloat16)


def draw_teacher_weight(key, part):
    query, other = rough_weight(jax.random.fold_in(key, 11), D_T, HEADS_T, HD_T)
    return jnp.stack([query, other], axis=1).reshape(D_T, 2, HEADS_T * HD_T).astype(jnp.bfloat16)


def draw_student_weight(key, part):
    query, other = rough_weight(jax.random.fold_in(key, 13), D_S, HEADS_S, HD_S)
    return jnp.stack([query, other], axis=2).reshape(D_S, HEADS_S * 2 * HD_S).astype(jnp.bfloat16)


def with_ends(entries, own_key, low, high):
    spot = [jax.random.randint(jax.random.fold_in(own_key, axis), (), 0, length) for axis, length in enumerate(entries.shape)]
    longest = entries.shape.index(max(entries.shape))
    next_to = spot[:longest] + [(spot[longest] + 1) % entries.shape[longest]] + spot[longest + 1:]
    return entries.at[tuple(spot)].set(low).at[tuple(next_to)].set(high)


def normal_values(own_key, shape, scale, bound, held_as=jnp.bfloat16):
    return jnp.clip(scale * jax.random.normal(own_key, shape, jnp.float32), -bound, bound).astype(held_as)


def setup_inputs(seed: int = 0, part: int = 0) -> dict:
    arg_keys = jax.random.split(jax.random.key(seed), 10)
    part_splits = jax.random.split(jax.random.fold_in(arg_keys[9], part), 10)
    teacher_input = draw_teacher_input(jax.random.fold_in(jax.random.fold_in(arg_keys[9], part), 71), part)
    teacher_gain = jnp.clip(jnp.exp(jax.random.uniform(arg_keys[1], (D_T,), jnp.float32, math.log(0.5), math.log(2.0))), 0.5, 2.0)
    teacher_weight = draw_teacher_weight(jax.random.fold_in(arg_keys[9], 71), part)
    head_counts = with_ends(jax.random.randint(arg_keys[3], (HEADS_T, HEADS_S), 0, 4), jax.random.fold_in(arg_keys[3], 1), 0, 3).astype(jnp.int32)
    assignment = jax.random.permutation(part_splits[4], IMAGES).astype(jnp.int32)
    student_input = draw_student_input(jax.random.fold_in(jax.random.fold_in(arg_keys[9], part), 71), part)
    student_gain = jnp.clip(jnp.exp(jax.random.uniform(arg_keys[6], (D_S,), jnp.float32, math.log(0.5), math.log(2.0))), 0.5, 2.0)
    student_bias = normal_values(arg_keys[7], (D_S,), 0.5, 3.0, jnp.float32)
    student_weight = draw_student_weight(jax.random.fold_in(arg_keys[9], 71), part)
    return dict(teacher_input=teacher_input, teacher_gain=teacher_gain, teacher_weight=teacher_weight, head_counts=head_counts, assignment=assignment, student_input=student_input, student_gain=student_gain, student_bias=student_bias, student_weight=student_weight)


def layer_norm(values, gain, shift):
    wide = values.astype(jnp.float32)
    center = wide - lax.optimization_barrier(jnp.mean(wide, axis=-1, keepdims=True))
    spread = lax.optimization_barrier(jnp.mean(center * center, axis=-1, keepdims=True))
    return center * lax.rsqrt(spread + 1e-06) * gain + shift

def reference(teacher_input, teacher_gain, teacher_weight, head_counts, assignment, student_input, student_gain, student_bias, student_weight):
    heads_dev = HEADS_T // N_TENSOR
    counts_grouped = head_counts.astype(jnp.float32).reshape(N_TENSOR, heads_dev, HEADS_S)

    def teacher_image(image):
        normed = layer_norm(image, teacher_gain, 0.0).astype(jnp.bfloat16)
        query = (jnp.dot(normed[:QROWS], teacher_weight[:, 0, :], preferred_element_type=jnp.float32) * HD_T ** (-0.5)).astype(jnp.bfloat16)
        keys = jnp.dot(normed, teacher_weight[:, 1, :], preferred_element_type=jnp.float32).astype(jnp.bfloat16)
        query = query.reshape(QROWS, HEADS_T, HD_T).astype(jnp.float32)
        keys = keys.reshape(TOKENS, HEADS_T, HD_T).astype(jnp.float32)
        scores = jnp.einsum('qhd,khd->hqk', query, keys)
        maps = jax.nn.softmax(scores, axis=-1).astype(jnp.bfloat16)
        grouped = maps.astype(jnp.float32).reshape(N_TENSOR, heads_dev, QROWS, TOKENS)
        partial_value = (jnp.einsum('tgqk,tgs->tsqk', grouped, counts_grouped) / DIVISOR).astype(jnp.bfloat16)
        partial_value = lax.optimization_barrier(partial_value)
        return lax.optimization_barrier(jnp.sum(partial_value.astype(jnp.float32), axis=0)).astype(jnp.bfloat16)
    folded = lax.map(teacher_image, teacher_input)
    packed = student_weight.reshape(D_S, HEADS_S, 2, HD_S)
    weight_query = packed[:, :, 0, :].reshape(D_S, HEADS_S * HD_S)
    weight_key = packed[:, :, 1, :].reshape(D_S, HEADS_S * HD_S)

    def student_image(total, slot):
        image = student_input[slot]
        target = lax.dynamic_index_in_dim(folded, assignment[slot].astype(jnp.int32), 0, keepdims=False).astype(jnp.float32)
        normed = layer_norm(image, student_gain, student_bias).astype(jnp.bfloat16)
        query = (jnp.dot(normed[:QROWS], weight_query, preferred_element_type=jnp.float32) * HD_S ** (-0.5)).astype(jnp.bfloat16)
        keys = jnp.dot(normed, weight_key, preferred_element_type=jnp.float32).astype(jnp.bfloat16)
        query = query.reshape(QROWS, HEADS_S, HD_S).astype(jnp.float32)
        keys = keys.reshape(TOKENS, HEADS_S, HD_S).astype(jnp.float32)
        probs = jax.nn.softmax(jnp.einsum('qhd,khd->hqk', query, keys), axis=-1)
        score_grad = (probs * lax.optimization_barrier(jnp.sum(target, axis=-1, keepdims=True)) - target).astype(jnp.bfloat16).astype(jnp.float32)
        query_grad = (jnp.einsum('hqk,khd->qhd', score_grad, keys) * HD_S ** (-0.5)).astype(jnp.bfloat16)
        key_grad = jnp.einsum('hqk,qhd->khd', score_grad, query).astype(jnp.bfloat16)
        grad_query = jnp.dot(normed[:QROWS].T, query_grad.reshape(QROWS, HEADS_S * HD_S), preferred_element_type=jnp.float32)
        grad_key = jnp.dot(normed.T, key_grad.reshape(TOKENS, HEADS_S * HD_S), preferred_element_type=jnp.float32)
        both = jnp.stack([grad_query.reshape(D_S, HEADS_S, HD_S), grad_key.reshape(D_S, HEADS_S, HD_S)], axis=2)
        return (total + both.reshape(D_S, HEADS_S * 2 * HD_S), None)
    start = jnp.zeros((D_S, HEADS_S * 2 * HD_S), jnp.float32)
    weight_grad, _ = lax.scan(student_image, start, jnp.arange(IMAGES, dtype=jnp.int32))
    return weight_grad
```

```python
import functools

import jax
import jax.numpy as jnp
from jax import lax
from jax.experimental import pallas as pl
from jax.experimental.pallas import tpu as pltpu
from jax.sharding import PartitionSpec as P

HD_T = 128
HD_S = 64
QROWS = 128
DIVISOR = 72
CORES = 2
MESH = pl.DeviceIdType.MESH


def layer_norm(values, gain, shift):
    wide = values.astype(jnp.float32)
    center = wide - jnp.mean(wide, axis=-1, keepdims=True)
    spread = jnp.mean(center * center, axis=-1, keepdims=True)
    return center * lax.rsqrt(spread + 1e-06) * gain + shift


def rounded_up(value, unit):
    return -(-value // unit) * unit


def teacher_kernel(
    sizes,
    counts_ref,
    x_ref,
    gain_ref,
    w_ref,
    out_ref,
    wbuf,
    normed,
    acc,
    part,
    landed,
    own_sem,
    sx,
    rx,
    sy,
    ry,
    so,
    ro,
    spx,
    rpx,
    spy,
    rpy,
    sz,
    rz,
):
    n_dp, n_group, n_tensor, heads_here, s_heads, images, tokens = sizes
    n_x = n_dp // CORES
    rows = w_ref.shape[1]
    rows_part = rows // n_group
    pad = normed.shape[0] // images
    s_here = s_heads // n_tensor

    dp = lax.axis_index("dp")
    y = lax.axis_index("group")
    t = lax.axis_index("tensor")
    x = dp // CORES
    core = lax.rem(dp, CORES)
    mate = x * CORES + (1 - core)

    def x_peer(s):
        return lax.rem(x + s, n_x) * CORES + core

    def x_source(s):
        return lax.rem(x + n_x - s, n_x) * CORES + core

    barrier = pltpu.get_barrier_semaphore()
    waits = 0
    for s in range(1, n_x):
        pl.semaphore_signal(barrier, inc=1, device_id={"dp": x_peer(s)}, device_id_type=MESH)
        waits += 1
    pl.semaphore_signal(barrier, inc=1, device_id={"dp": mate}, device_id_type=MESH)
    waits += 1
    for s in range(1, n_group):
        pl.semaphore_signal(
            barrier, inc=1, device_id={"group": lax.rem(y + s, n_group)}, device_id_type=MESH
        )
        waits += 1
    for s in range(1, n_tensor):
        pl.semaphore_signal(
            barrier, inc=1, device_id={"tensor": lax.rem(t + s, n_tensor)}, device_id_type=MESH
        )
        waits += 1
    pl.semaphore_wait(barrier, waits)

    def cols(k):
        return pl.ds(pl.multiple_of(k * HD_T, HD_T), HD_T)

    def band(g):
        return pl.ds(pl.multiple_of(g * rows_part, 16), rows_part)

    def copy_x(k, s):
        return pltpu.make_async_remote_copy(
            src_ref=w_ref.at[:, band(y), cols(k)],
            dst_ref=wbuf.at[dp, :, band(y), cols(k)],
            send_sem=sx.at[k, s - 1],
            recv_sem=rx.at[k, s - 1],
            device_id={"dp": x_peer(s)},
            device_id_type=MESH,
        )

    def copy_own(k):
        return pltpu.make_async_remote_copy(
            src_ref=w_ref.at[:, :, cols(k)],
            dst_ref=wbuf.at[dp, :, :, cols(k)],
            send_sem=so.at[k],
            recv_sem=ro.at[k],
            device_id={"dp": mate},
            device_id_type=MESH,
        )

    def copy_y(k, s, g):
        where = (x_source(s), slice(None), band(y), cols(k))
        return pltpu.make_async_remote_copy(
            src_ref=wbuf.at[where],
            dst_ref=wbuf.at[where],
            send_sem=sy.at[k, s - 1, g - 1],
            recv_sem=ry.at[k, s - 1, g - 1],
            device_id={"group": lax.rem(y + g, n_group)},
            device_id_type=MESH,
        )

    def copy_mate_x(k, s):
        where = (x_source(s), slice(None), band(y), cols(k))
        return pltpu.make_async_remote_copy(
            src_ref=wbuf.at[where],
            dst_ref=wbuf.at[where],
            send_sem=spx.at[k, s - 1],
            recv_sem=rpx.at[k, s - 1],
            device_id={"dp": mate},
            device_id_type=MESH,
        )

    def copy_mate_y(k, s, g):
        where = (x_source(s), slice(None), band(lax.rem(y + n_group - g, n_group)), cols(k))
        return pltpu.make_async_remote_copy(
            src_ref=wbuf.at[where],
            dst_ref=wbuf.at[where],
            send_sem=spy.at[k, s - 1, g - 1],
            recv_sem=rpy.at[k, s - 1, g - 1],
            device_id={"dp": mate},
            device_id_type=MESH,
        )

    def open_sends(k, carry):
        for s in range(1, n_x):
            copy_x(k, s).start()
        copy_own(k).start()
        return carry

    lax.fori_loop(0, heads_here, open_sends, 0)
    own_copy = pltpu.make_async_copy(w_ref, wbuf.at[dp], own_sem)
    own_copy.start()

    gain = gain_ref[...]
    for i in range(images):

        def norm_rows(r, carry):
            block = layer_norm(x_ref[i, pl.ds(pl.multiple_of(r * 16, 16), 16), :], gain, 0.0)
            normed[pl.ds(pl.multiple_of(i * pad + r * 16, 16), 16), :] = block.astype(jnp.bfloat16)
            return carry

        whole = tokens // 16
        lax.fori_loop(0, whole, norm_rows, 0)
        rest = tokens - whole * 16
        if rest:
            last = layer_norm(x_ref[i, whole * 16 : tokens, :], gain, 0.0)
            normed[i * pad + whole * 16 : (i + 1) * pad, :] = jnp.concatenate(
                [last, jnp.zeros((16 - rest, last.shape[1]), jnp.float32)], axis=0
            ).astype(jnp.bfloat16)
    acc[...] = jnp.zeros_like(acc)
    own_copy.wait()

    def attend(k):
        keys = jnp.zeros((images * pad, HD_T), jnp.float32)
        query = jnp.zeros((images * QROWS, HD_T), jnp.float32)
        for d in range(n_dp):
            deep = slice(d * rows, (d + 1) * rows)
            keys += jnp.dot(
                normed[:, deep], wbuf[d, 1, :, cols(k)], preferred_element_type=jnp.float32
            )
            front = jnp.concatenate(
                [normed[i * pad : i * pad + QROWS, deep] for i in range(images)], axis=0
            )
            query += jnp.dot(front, wbuf[d, 0, :, cols(k)], preferred_element_type=jnp.float32)
        query = (query * HD_T ** (-0.5)).astype(jnp.bfloat16)
        keys = keys.astype(jnp.bfloat16)
        for i in range(images):
            scores = lax.dot_general(
                keys[i * pad : (i + 1) * pad],
                query[i * QROWS : (i + 1) * QROWS],
                (((1,), (1,)), ((), ())),
                preferred_element_type=jnp.float32,
            )
            spot = lax.broadcasted_iota(jnp.int32, scores.shape, 0)
            scores = jnp.where(spot < tokens, scores, -jnp.inf)
            power = jnp.exp(scores - jnp.max(scores, axis=0, keepdims=True))
            maps = power / jnp.sum(power, axis=0, keepdims=True)
            maps = maps.astype(jnp.bfloat16).astype(jnp.float32)
            for s in range(s_heads):
                count = counts_ref[t * heads_here + k, s].astype(jnp.float32)
                acc[s, i] += count * maps

    def step(k, carry):
        @pl.when(k < heads_here)
        def _():
            for s in range(1, n_x):
                copy_x(k, s).wait_recv()
                for g in range(1, n_group):
                    copy_y(k, s, g).start()
                copy_mate_x(k, s).start()

        @pl.when(k > 0)
        def _():
            j = k - 1
            for s in range(1, n_x):
                for g in range(1, n_group):
                    copy_y(j, s, g).wait_recv()
                    copy_mate_y(j, s, g).start()
            copy_own(j).wait_recv()
            for s in range(1, n_x):
                copy_mate_x(j, s).wait_recv()
                for g in range(1, n_group):
                    copy_mate_y(j, s, g).wait_recv()
            attend(j)

        return carry

    lax.fori_loop(0, heads_here + 1, step, 0)

    def copy_z(s):
        to = lax.rem(t + s, n_tensor)
        return pltpu.make_async_remote_copy(
            src_ref=part.at[pl.ds(to * s_here, s_here)],
            dst_ref=landed.at[s - 1],
            send_sem=sz.at[s - 1],
            recv_sem=rz.at[s - 1],
            device_id={"tensor": to},
            device_id_type=MESH,
        )

    part[...] = (acc[...] / DIVISOR).astype(jnp.bfloat16)
    for s in range(n_tensor - 1, 0, -1):
        copy_z(s).start()

    def drain(k, carry):
        for s in range(1, n_x):
            copy_x(k, s).wait_send()
            copy_mate_x(k, s).wait_send()
            for g in range(1, n_group):
                copy_y(k, s, g).wait_send()
                copy_mate_y(k, s, g).wait_send()
        copy_own(k).wait_send()
        return carry

    lax.fori_loop(0, heads_here, drain, 0)
    for s in range(1, n_tensor):
        copy_z(s).wait()
    for h in range(s_here):
        total = part[t * s_here + h].astype(jnp.float32)
        for s in range(1, n_tensor):
            total += landed[s - 1, h].astype(jnp.float32)
        out_ref[h] = total.astype(jnp.bfloat16)


def teacher_folded(mesh_sizes, teacher_input, teacher_gain, teacher_weight, head_counts):
    n_dp, n_group, n_tensor = mesh_sizes
    images, tokens, width = teacher_input.shape
    rows, _, width_here = teacher_weight.shape
    heads_here = width_here // HD_T
    s_heads = head_counts.shape[1]
    s_here = s_heads // n_tensor
    pad = rounded_up(tokens, 16)
    n_x = n_dp // CORES
    split = jnp.transpose(teacher_weight, (1, 0, 2))
    sizes = (n_dp, n_group, n_tensor, heads_here, s_heads, images, tokens)
    dma = pltpu.SemaphoreType.DMA
    one = (heads_here, max(n_x - 1, 1))
    two = one + (max(n_group - 1, 1),)
    return pl.pallas_call(
        functools.partial(teacher_kernel, sizes),
        out_shape=jax.ShapeDtypeStruct((s_here, images, pad, QROWS), jnp.bfloat16),
        in_specs=[
            pl.BlockSpec(memory_space=pltpu.SMEM),
            pl.BlockSpec(memory_space=pltpu.VMEM),
            pl.BlockSpec(memory_space=pltpu.VMEM),
            pl.BlockSpec(memory_space=pl.ANY),
        ],
        out_specs=pl.BlockSpec(memory_space=pltpu.VMEM),
        scratch_shapes=[
            pltpu.VMEM((n_dp, 2, rows, width_here), jnp.bfloat16),
            pltpu.VMEM((images * pad, width), jnp.bfloat16),
            pltpu.VMEM((s_heads, images, pad, QROWS), jnp.float32),
            pltpu.VMEM((s_heads, images, pad, QROWS), jnp.bfloat16),
            pltpu.VMEM((max(n_tensor - 1, 1), s_here, images, pad, QROWS), jnp.bfloat16),
            dma,
            dma(one),
            dma(one),
            dma(two),
            dma(two),
            dma((heads_here,)),
            dma((heads_here,)),
            dma(one),
            dma(one),
            dma(two),
            dma(two),
            dma((max(n_tensor - 1, 1),)),
            dma((max(n_tensor - 1, 1),)),
        ],
        compiler_params=pltpu.CompilerParams(
            collective_id=0, has_side_effects=True, vmem_limit_bytes=67043328
        ),
    )(head_counts, teacher_input, teacher_gain.reshape(1, width), split)


def sum_over_dp(local, n_dp):
    half = local.shape[0] // CORES
    core = lax.rem(lax.axis_index("dp"), CORES)
    mates = [(d, d ^ 1) for d in range(n_dp)]
    rounded = local.astype(jnp.bfloat16)
    mine = lax.dynamic_slice_in_dim(local, core * half, half, 0)
    other = lax.dynamic_slice_in_dim(rounded, (1 - core) * half, half, 0)
    mine = mine + lax.ppermute(other, "dp", mates).astype(jnp.float32)
    sent = mine.astype(jnp.bfloat16)
    for s in range(1, n_dp // CORES):
        around = [(d, (d + CORES * s) % n_dp) for d in range(n_dp)]
        mine = mine + lax.ppermute(sent, "dp", around).astype(jnp.float32)
    done = mine.astype(jnp.bfloat16)
    theirs = lax.ppermute(done, "dp", mates)
    first = jnp.where(core == 0, done, theirs)
    second = jnp.where(core == 0, theirs, done)
    return jnp.concatenate([first, second], axis=0).astype(jnp.float32)


def on_device(
    mesh_sizes,
    teacher_input,
    teacher_gain,
    teacher_weight,
    head_counts,
    assignment,
    student_input,
    student_gain,
    student_bias,
    student_weight,
):
    images, tokens, width_s = student_input.shape
    student_heads = student_weight.shape[1] // (2 * HD_S)
    folded = teacher_folded(mesh_sizes, teacher_input, teacher_gain, teacher_weight, head_counts)
    piece = lax.all_gather(folded, "dp", axis=1, tiled=True)
    width_piece = piece.shape[1]
    positions = jnp.arange(width_piece, dtype=jnp.int32)
    picker = (assignment[:, None] == positions[None, :]).astype(jnp.bfloat16)
    target = jnp.einsum("ji,hikq->hjkq", picker, piece, preferred_element_type=jnp.float32)
    target_wide = target.astype(jnp.bfloat16).astype(jnp.float32)[:, :, :tokens]
    student_normed = layer_norm(student_input, student_gain, student_bias).astype(jnp.bfloat16)
    normed_front = student_normed[:, :QROWS]
    packed = student_weight.reshape(width_s, student_heads, 2, HD_S)
    weight_query = packed[:, :, 0, :].reshape(width_s, student_heads * HD_S)
    weight_key = packed[:, :, 1, :].reshape(width_s, student_heads * HD_S)
    student_query = (
        jnp.einsum("btd,dc->btc", normed_front, weight_query, preferred_element_type=jnp.float32)
        * HD_S ** (-0.5)
    ).astype(jnp.bfloat16)
    student_keys = jnp.einsum(
        "btd,dc->btc", student_normed, weight_key, preferred_element_type=jnp.float32
    ).astype(jnp.bfloat16)
    split_query = student_query.reshape(images, QROWS, student_heads, HD_S)
    split_keys = student_keys.reshape(images, tokens, student_heads, HD_S)
    probs = jax.nn.softmax(
        jnp.einsum("bqhd,bkhd->hbkq", split_query, split_keys, preferred_element_type=jnp.float32),
        axis=2,
    )
    score_grad = (probs * jnp.sum(target_wide, axis=2, keepdims=True) - target_wide).astype(
        jnp.bfloat16
    )
    query_grad = (
        jnp.einsum("hbkq,bkhd->bqhd", score_grad, split_keys, preferred_element_type=jnp.float32)
        * HD_S ** (-0.5)
    ).astype(jnp.bfloat16)
    key_grad = jnp.einsum(
        "hbkq,bqhd->bkhd", score_grad, split_query, preferred_element_type=jnp.float32
    ).astype(jnp.bfloat16)
    grad_query = jnp.einsum(
        "fkm,fkp->mp",
        normed_front,
        query_grad.reshape(images, QROWS, student_heads * HD_S),
        preferred_element_type=jnp.float32,
    )
    grad_key = jnp.einsum(
        "oip,ois->ps",
        student_normed,
        key_grad.reshape(images, tokens, student_heads * HD_S),
        preferred_element_type=jnp.float32,
    )
    local_grad = jnp.stack(
        [
            grad_query.reshape(width_s, student_heads, HD_S),
            grad_key.reshape(width_s, student_heads, HD_S),
        ],
        axis=2,
    )
    local_grad = local_grad.reshape(width_s, student_heads * 2 * HD_S)
    return sum_over_dp(local_grad, mesh_sizes[0])


def solution(mesh):
    placed = (
        P(("group", "dp"), None, None),
        P(),
        P("dp", None, "tensor"),
        P(),
        P(("group", "dp")),
        P(("group", "dp"), None, None),
        P(),
        P(),
        P(None, "tensor"),
    )
    mesh_sizes = (mesh.shape["dp"], mesh.shape["group"], mesh.shape["tensor"])
    return jax.shard_map(
        functools.partial(on_device, mesh_sizes),
        mesh=mesh,
        in_specs=placed,
        out_specs=P("group", "tensor"),
        check_vma=False,
    )
```

```python
import functools

import jax
import jax.numpy as jnp
from jax import lax
from jax.experimental import pallas as pl
from jax.experimental.pallas import tpu as pltpu
from jax.sharding import PartitionSpec as P

HD_T = 128
HD_S = 64
QROWS = 128
DIVISOR = 72
CORES = 2
MESH = pl.DeviceIdType.MESH


def layer_norm(values, gain, shift):
    wide = values.astype(jnp.float32)
    center = wide - jnp.mean(wide, axis=-1, keepdims=True)
    spread = jnp.mean(center * center, axis=-1, keepdims=True)
    return center * lax.rsqrt(spread + 1e-06) * gain + shift


def rounded_up(value, unit):
    return -(-value // unit) * unit


def teacher_kernel(
    sizes,
    counts_ref,
    slots_ref,
    x_ref,
    gain_ref,
    w_ref,
    out_ref,
    wbuf,
    normed,
    acc,
    part,
    landed,
    gathered,
    own_sem,
    sx,
    rx,
    sy,
    ry,
    so,
    ro,
    spx,
    rpx,
    spy,
    rpy,
    sz,
    rz,
    sg,
    rg,
):
    n_dp, n_group, n_tensor, heads_here, s_heads, images, tokens = sizes
    n_x = n_dp // CORES
    rows = w_ref.shape[1]
    rows_part = rows // n_group
    pad = normed.shape[0] // images
    s_here = s_heads // n_tensor

    dp = lax.axis_index("dp")
    y = lax.axis_index("group")
    t = lax.axis_index("tensor")
    x = dp // CORES
    core = lax.rem(dp, CORES)
    mate = x * CORES + (1 - core)

    def x_peer(s):
        return lax.rem(x + s, n_x) * CORES + core

    def x_source(s):
        return lax.rem(x + n_x - s, n_x) * CORES + core

    barrier = pltpu.get_barrier_semaphore()
    waits = 0
    for s in range(1, n_dp):
        pl.semaphore_signal(
            barrier, inc=1, device_id={"dp": lax.rem(dp + s, n_dp)}, device_id_type=MESH
        )
        waits += 1
    for s in range(1, n_group):
        pl.semaphore_signal(
            barrier, inc=1, device_id={"group": lax.rem(y + s, n_group)}, device_id_type=MESH
        )
        waits += 1
    for s in range(1, n_tensor):
        pl.semaphore_signal(
            barrier, inc=1, device_id={"tensor": lax.rem(t + s, n_tensor)}, device_id_type=MESH
        )
        waits += 1
    pl.semaphore_wait(barrier, waits)

    def cols(k):
        return pl.ds(pl.multiple_of(k * HD_T, HD_T), HD_T)

    def band(g):
        return pl.ds(pl.multiple_of(g * rows_part, 16), rows_part)

    def copy_x(k, s):
        return pltpu.make_async_remote_copy(
            src_ref=w_ref.at[:, band(y), cols(k)],
            dst_ref=wbuf.at[dp, :, band(y), cols(k)],
            send_sem=sx.at[k, s - 1],
            recv_sem=rx.at[k, s - 1],
            device_id={"dp": x_peer(s)},
            device_id_type=MESH,
        )

    def copy_own(k):
        return pltpu.make_async_remote_copy(
            src_ref=w_ref.at[:, :, cols(k)],
            dst_ref=wbuf.at[dp, :, :, cols(k)],
            send_sem=so.at[k],
            recv_sem=ro.at[k],
            device_id={"dp": mate},
            device_id_type=MESH,
        )

    def copy_y(k, s, g):
        where = (x_source(s), slice(None), band(y), cols(k))
        return pltpu.make_async_remote_copy(
            src_ref=wbuf.at[where],
            dst_ref=wbuf.at[where],
            send_sem=sy.at[k, s - 1, g - 1],
            recv_sem=ry.at[k, s - 1, g - 1],
            device_id={"group": lax.rem(y + g, n_group)},
            device_id_type=MESH,
        )

    def copy_mate_x(k, s):
        where = (x_source(s), slice(None), band(y), cols(k))
        return pltpu.make_async_remote_copy(
            src_ref=wbuf.at[where],
            dst_ref=wbuf.at[where],
            send_sem=spx.at[k, s - 1],
            recv_sem=rpx.at[k, s - 1],
            device_id={"dp": mate},
            device_id_type=MESH,
        )

    def copy_mate_y(k, s, g):
        where = (x_source(s), slice(None), band(lax.rem(y + n_group - g, n_group)), cols(k))
        return pltpu.make_async_remote_copy(
            src_ref=wbuf.at[where],
            dst_ref=wbuf.at[where],
            send_sem=spy.at[k, s - 1, g - 1],
            recv_sem=rpy.at[k, s - 1, g - 1],
            device_id={"dp": mate},
            device_id_type=MESH,
        )

    def open_sends(k, carry):
        for s in range(1, n_x):
            copy_x(k, s).start()
        copy_own(k).start()
        return carry

    lax.fori_loop(0, heads_here, open_sends, 0)
    own_copy = pltpu.make_async_copy(w_ref, wbuf.at[dp], own_sem)
    own_copy.start()

    acc[...] = jnp.zeros_like(acc)
    own_copy.wait()

    def norm_image(i):
        gain = gain_ref[...]

        def norm_rows(r, carry):
            block = layer_norm(x_ref[i, pl.ds(pl.multiple_of(r * 16, 16), 16), :], gain, 0.0)
            normed[pl.ds(pl.multiple_of(i * pad + r * 16, 16), 16), :] = block.astype(jnp.bfloat16)
            return carry

        whole = tokens // 16
        lax.fori_loop(0, whole, norm_rows, 0)
        rest = tokens - whole * 16
        if rest:
            last = layer_norm(x_ref[i, whole * 16 : tokens, :], gain, 0.0)
            normed[pl.ds(pl.multiple_of(i * pad + whole * 16, 16), 16), :] = jnp.concatenate(
                [last, jnp.zeros((16 - rest, last.shape[1]), jnp.float32)], axis=0
            ).astype(jnp.bfloat16)

    def attend(k):
        keys = jnp.zeros((images * pad, HD_T), jnp.float32)
        query = jnp.zeros((images * QROWS, HD_T), jnp.float32)
        for d in range(n_dp):
            deep = slice(d * rows, (d + 1) * rows)
            keys += jnp.dot(
                normed[:, deep], wbuf[d, 1, :, cols(k)], preferred_element_type=jnp.float32
            )
            front = jnp.concatenate(
                [normed[i * pad : i * pad + QROWS, deep] for i in range(images)], axis=0
            )
            query += jnp.dot(front, wbuf[d, 0, :, cols(k)], preferred_element_type=jnp.float32)
        query = (query * HD_T ** (-0.5)).astype(jnp.bfloat16)
        keys = keys.astype(jnp.bfloat16)
        for i in range(images):
            scores = lax.dot_general(
                keys[i * pad : (i + 1) * pad],
                query[i * QROWS : (i + 1) * QROWS],
                (((1,), (1,)), ((), ())),
                preferred_element_type=jnp.float32,
            )
            spot = lax.broadcasted_iota(jnp.int32, scores.shape, 0)
            scores = jnp.where(spot < tokens, scores, -jnp.inf)
            power = jnp.exp(scores - jnp.max(scores, axis=0, keepdims=True))
            maps = power / jnp.sum(power, axis=0, keepdims=True)
            maps = maps.astype(jnp.bfloat16).astype(jnp.float32)
            for s in range(s_heads):
                count = counts_ref[t * heads_here + k, s].astype(jnp.float32)
                acc[s, i] += count * maps

    def step(k, carry):
        @pl.when(k < heads_here)
        def _():
            for s in range(1, n_x):
                copy_x(k, s).wait_recv()
                for g in range(1, n_group):
                    copy_y(k, s, g).start()
                copy_mate_x(k, s).start()

        @pl.when(k > 0)
        def _():
            j = k - 1
            for s in range(1, n_x):
                for g in range(1, n_group):
                    copy_y(j, s, g).wait_recv()
                    copy_mate_y(j, s, g).start()

        @pl.when(k < images)
        def _():
            norm_image(k)

        def ready(j, inner):
            copy_own(j).wait_recv()
            for s in range(1, n_x):
                copy_mate_x(j, s).wait_recv()
                for g in range(1, n_group):
                    copy_mate_y(j, s, g).wait_recv()
            attend(j)
            return inner

        lax.fori_loop(
            jnp.where(k <= images, 0, k - 1), jnp.where(k < images, 0, k), ready, 0
        )
        return carry

    lax.fori_loop(0, heads_here + 1, step, 0)

    def copy_z(s, h):
        to = lax.rem(t + s, n_tensor)
        return pltpu.make_async_remote_copy(
            src_ref=part.at[to * s_here + h],
            dst_ref=landed.at[s - 1, h],
            send_sem=sz.at[s - 1, h],
            recv_sem=rz.at[s - 1, h],
            device_id={"tensor": to},
            device_id_type=MESH,
        )

    def copy_dp(s, h):
        own = gathered.at[h, pl.ds(dp * images, images)]
        return pltpu.make_async_remote_copy(
            src_ref=own,
            dst_ref=own,
            send_sem=sg.at[s - 1, h],
            recv_sem=rg.at[s - 1, h],
            device_id={"dp": lax.rem(dp + s, n_dp)},
            device_id_type=MESH,
        )

    for h in range(s_here):
        for s in range(1, n_tensor):
            spot = lax.rem(t + s, n_tensor) * s_here + h
            part[spot] = (acc[spot] / DIVISOR).astype(jnp.bfloat16)
            copy_z(s, h).start()
    for h in range(s_here):
        total = (acc[t * s_here + h] / DIVISOR).astype(jnp.bfloat16).astype(jnp.float32)
        for s in range(1, n_tensor):
            copy_z(s, h).wait_recv()
            total += landed[s - 1, h].astype(jnp.float32)
        gathered[h, pl.ds(dp * images, images)] = total.astype(jnp.bfloat16)
        for s in range(1, n_dp):
            copy_dp(s, h).start()

    def drain(k, carry):
        for s in range(1, n_x):
            copy_x(k, s).wait_send()
            copy_mate_x(k, s).wait_send()
            for g in range(1, n_group):
                copy_y(k, s, g).wait_send()
                copy_mate_y(k, s, g).wait_send()
        copy_own(k).wait_send()
        return carry

    lax.fori_loop(0, heads_here, drain, 0)
    for h in range(s_here):
        for s in range(1, n_tensor):
            copy_z(s, h).wait_send()
        for s in range(1, n_dp):
            copy_dp(s, h).wait()
    for h in range(s_here):
        for j in range(images):
            out_ref[h, j] = gathered[h, slots_ref[j]]


def teacher_folded(mesh_sizes, teacher_input, teacher_gain, teacher_weight, head_counts, assignment):
    n_dp, n_group, n_tensor = mesh_sizes
    images, tokens, width = teacher_input.shape
    rows, _, width_here = teacher_weight.shape
    heads_here = width_here // HD_T
    s_heads = head_counts.shape[1]
    s_here = s_heads // n_tensor
    pad = rounded_up(tokens, 16)
    n_x = n_dp // CORES
    split = jnp.transpose(teacher_weight, (1, 0, 2))
    sizes = (n_dp, n_group, n_tensor, heads_here, s_heads, images, tokens)
    dma = pltpu.SemaphoreType.DMA
    one = (heads_here, max(n_x - 1, 1))
    two = one + (max(n_group - 1, 1),)
    return pl.pallas_call(
        functools.partial(teacher_kernel, sizes),
        out_shape=jax.ShapeDtypeStruct((s_here, images, pad, QROWS), jnp.bfloat16),
        in_specs=[
            pl.BlockSpec(memory_space=pltpu.SMEM),
            pl.BlockSpec(memory_space=pltpu.SMEM),
            pl.BlockSpec(memory_space=pltpu.VMEM),
            pl.BlockSpec(memory_space=pltpu.VMEM),
            pl.BlockSpec(memory_space=pl.ANY),
        ],
        out_specs=pl.BlockSpec(memory_space=pltpu.VMEM),
        scratch_shapes=[
            pltpu.VMEM((n_dp, 2, rows, width_here), jnp.bfloat16),
            pltpu.VMEM((images * pad, width), jnp.bfloat16),
            pltpu.VMEM((s_heads, images, pad, QROWS), jnp.float32),
            pltpu.VMEM((s_heads, images, pad, QROWS), jnp.bfloat16),
            pltpu.VMEM((max(n_tensor - 1, 1), s_here, images, pad, QROWS), jnp.bfloat16),
            pltpu.VMEM((s_here, n_dp * images, pad, QROWS), jnp.bfloat16),
            dma,
            dma(one),
            dma(one),
            dma(two),
            dma(two),
            dma((heads_here,)),
            dma((heads_here,)),
            dma(one),
            dma(one),
            dma(two),
            dma(two),
            dma((max(n_tensor - 1, 1), s_here)),
            dma((max(n_tensor - 1, 1), s_here)),
            dma((n_dp - 1, s_here)),
            dma((n_dp - 1, s_here)),
        ],
        compiler_params=pltpu.CompilerParams(
            collective_id=0, has_side_effects=True, vmem_limit_bytes=67043328
        ),
    )(head_counts, assignment, teacher_input, teacher_gain.reshape(1, width), split)


def sum_over_dp(local, n_dp):
    half = local.shape[0] // CORES
    core = lax.rem(lax.axis_index("dp"), CORES)
    mates = [(d, d ^ 1) for d in range(n_dp)]
    rounded = local.astype(jnp.bfloat16)
    mine = lax.dynamic_slice_in_dim(local, core * half, half, 0)
    other = lax.dynamic_slice_in_dim(rounded, (1 - core) * half, half, 0)
    mine = mine + lax.ppermute(other, "dp", mates).astype(jnp.float32)
    sent = mine.astype(jnp.bfloat16)
    for s in range(1, n_dp // CORES):
        around = [(d, (d + CORES * s) % n_dp) for d in range(n_dp)]
        mine = mine + lax.ppermute(sent, "dp", around).astype(jnp.float32)
    done = mine.astype(jnp.bfloat16)
    theirs = lax.ppermute(done, "dp", mates)
    first = jnp.where(core == 0, done, theirs)
    second = jnp.where(core == 0, theirs, done)
    return jnp.concatenate([first, second], axis=0).astype(jnp.float32)


def on_device(
    mesh_sizes,
    teacher_input,
    teacher_gain,
    teacher_weight,
    head_counts,
    assignment,
    student_input,
    student_gain,
    student_bias,
    student_weight,
):
    images, tokens, width_s = student_input.shape
    student_heads = student_weight.shape[1] // (2 * HD_S)
    target = teacher_folded(
        mesh_sizes, teacher_input, teacher_gain, teacher_weight, head_counts, assignment
    )
    target_wide = target.astype(jnp.float32)[:, :, :tokens]
    student_normed = layer_norm(student_input, student_gain, student_bias).astype(jnp.bfloat16)
    normed_front = student_normed[:, :QROWS]
    packed = student_weight.reshape(width_s, student_heads, 2, HD_S)
    weight_query = packed[:, :, 0, :].reshape(width_s, student_heads * HD_S)
    weight_key = packed[:, :, 1, :].reshape(width_s, student_heads * HD_S)
    student_query = (
        jnp.einsum("btd,dc->btc", normed_front, weight_query, preferred_element_type=jnp.float32)
        * HD_S ** (-0.5)
    ).astype(jnp.bfloat16)
    student_keys = jnp.einsum(
        "btd,dc->btc", student_normed, weight_key, preferred_element_type=jnp.float32
    ).astype(jnp.bfloat16)
    split_query = student_query.reshape(images, QROWS, student_heads, HD_S)
    split_keys = student_keys.reshape(images, tokens, student_heads, HD_S)
    probs = jax.nn.softmax(
        jnp.einsum("bqhd,bkhd->hbkq", split_query, split_keys, preferred_element_type=jnp.float32),
        axis=2,
    )
    score_grad = (probs * jnp.sum(target_wide, axis=2, keepdims=True) - target_wide).astype(
        jnp.bfloat16
    )
    query_grad = (
        jnp.einsum("hbkq,bkhd->bqhd", score_grad, split_keys, preferred_element_type=jnp.float32)
        * HD_S ** (-0.5)
    ).astype(jnp.bfloat16)
    key_grad = jnp.einsum(
        "hbkq,bqhd->bkhd", score_grad, split_query, preferred_element_type=jnp.float32
    ).astype(jnp.bfloat16)
    grad_query = jnp.einsum(
        "fkm,fkp->mp",
        normed_front,
        query_grad.reshape(images, QROWS, student_heads * HD_S),
        preferred_element_type=jnp.float32,
    )
    grad_key = jnp.einsum(
        "oip,ois->ps",
        student_normed,
        key_grad.reshape(images, tokens, student_heads * HD_S),
        preferred_element_type=jnp.float32,
    )
    local_grad = jnp.stack(
        [
            grad_query.reshape(width_s, student_heads, HD_S),
            grad_key.reshape(width_s, student_heads, HD_S),
        ],
        axis=2,
    )
    local_grad = local_grad.reshape(width_s, student_heads * 2 * HD_S)
    return sum_over_dp(local_grad, mesh_sizes[0])


def solution(mesh):
    placed = (
        P(("group", "dp"), None, None),
        P(),
        P("dp", None, "tensor"),
        P(),
        P(("group", "dp")),
        P(("group", "dp"), None, None),
        P(),
        P(),
        P(None, "tensor"),
    )
    mesh_sizes = (mesh.shape["dp"], mesh.shape["group"], mesh.shape["tensor"])
    return jax.shard_map(
        functools.partial(on_device, mesh_sizes),
        mesh=mesh,
        in_specs=placed,
        out_specs=P("group", "tensor"),
        check_vma=False,
    )
```

```python
import functools

import jax
import jax.numpy as jnp
from jax import lax
from jax.experimental import pallas as pl
from jax.experimental.pallas import tpu as pltpu
from jax.sharding import PartitionSpec as P

HD_T = 128
HD_S = 64
QROWS = 128
DIVISOR = 72
CORES = 2
MESH = pl.DeviceIdType.MESH


def layer_norm(values, gain, shift):
    wide = values.astype(jnp.float32)
    center = wide - jnp.mean(wide, axis=-1, keepdims=True)
    spread = jnp.mean(center * center, axis=-1, keepdims=True)
    return center * lax.rsqrt(spread + 1e-06) * gain + shift


def rounded_up(value, unit):
    return -(-value // unit) * unit


def teacher_kernel(
    sizes,
    counts_ref,
    slots_ref,
    x_ref,
    gain_ref,
    w_ref,
    out_ref,
    wbuf,
    normed,
    stage,
    acc,
    made,
    landed,
    fold,
    gathered,
    stage_sem,
    own_sem,
    sx,
    rx,
    sy,
    ry,
    so,
    ro,
    spx,
    rpx,
    spy,
    rpy,
    sz,
    rz,
    sf,
    rf,
    sg,
    rg,
    sm,
    rm,
):
    n_dp, n_group, n_tensor, heads_here, s_heads, images, tokens = sizes
    n_x = n_dp // CORES
    rows = w_ref.shape[1]
    rows_part = rows // n_group
    pad = normed.shape[0] // images
    s_here = s_heads // n_tensor
    per_image = n_tensor // images
    s_part = s_heads // per_image

    dp = lax.axis_index("dp")
    y = lax.axis_index("group")
    t = lax.axis_index("tensor")
    x = dp // CORES
    core = lax.rem(dp, CORES)
    mate = x * CORES + (1 - core)
    my_image = t // per_image
    my_part = lax.rem(t, per_image)

    def x_peer(s):
        return lax.rem(x + s, n_x) * CORES + core

    def x_source(s):
        return lax.rem(x + n_x - s, n_x) * CORES + core

    barrier = pltpu.get_barrier_semaphore()
    waits = 0
    for s in range(1, n_dp):
        pl.semaphore_signal(
            barrier, inc=1, device_id={"dp": lax.rem(dp + s, n_dp)}, device_id_type=MESH
        )
        waits += 1
    for s in range(1, n_group):
        pl.semaphore_signal(
            barrier, inc=1, device_id={"group": lax.rem(y + s, n_group)}, device_id_type=MESH
        )
        waits += 1
    for s in range(1, n_tensor):
        pl.semaphore_signal(
            barrier, inc=1, device_id={"tensor": lax.rem(t + s, n_tensor)}, device_id_type=MESH
        )
        waits += 1
    pl.semaphore_wait(barrier, waits)

    def cols(k):
        return pl.ds(pl.multiple_of(k * HD_T, HD_T), HD_T)

    def band(g):
        return pl.ds(pl.multiple_of(g * rows_part, 16), rows_part)

    def copy_x(k, s):
        return pltpu.make_async_remote_copy(
            src_ref=w_ref.at[:, band(y), cols(k)],
            dst_ref=wbuf.at[dp, :, band(y), cols(k)],
            send_sem=sx.at[k, s - 1],
            recv_sem=rx.at[k, s - 1],
            device_id={"dp": x_peer(s)},
            device_id_type=MESH,
        )

    def copy_own(k):
        return pltpu.make_async_remote_copy(
            src_ref=w_ref.at[:, :, cols(k)],
            dst_ref=wbuf.at[dp, :, :, cols(k)],
            send_sem=so.at[k],
            recv_sem=ro.at[k],
            device_id={"dp": mate},
            device_id_type=MESH,
        )

    def copy_y(k, s, g):
        where = (x_source(s), slice(None), band(y), cols(k))
        return pltpu.make_async_remote_copy(
            src_ref=wbuf.at[where],
            dst_ref=wbuf.at[where],
            send_sem=sy.at[k, s - 1, g - 1],
            recv_sem=ry.at[k, s - 1, g - 1],
            device_id={"group": lax.rem(y + g, n_group)},
            device_id_type=MESH,
        )

    def copy_mate_x(k, s):
        where = (x_source(s), slice(None), band(y), cols(k))
        return pltpu.make_async_remote_copy(
            src_ref=wbuf.at[where],
            dst_ref=wbuf.at[where],
            send_sem=spx.at[k, s - 1],
            recv_sem=rpx.at[k, s - 1],
            device_id={"dp": mate},
            device_id_type=MESH,
        )

    def copy_mate_y(k, s, g):
        where = (x_source(s), slice(None), band(lax.rem(y + n_group - g, n_group)), cols(k))
        return pltpu.make_async_remote_copy(
            src_ref=wbuf.at[where],
            dst_ref=wbuf.at[where],
            send_sem=spy.at[k, s - 1, g - 1],
            recv_sem=rpy.at[k, s - 1, g - 1],
            device_id={"dp": mate},
            device_id_type=MESH,
        )

    def open_sends(k, carry):
        for s in range(1, n_x):
            copy_x(k, s).start()
        copy_own(k).start()
        return carry

    lax.fori_loop(0, heads_here, open_sends, 0)
    own_copy = pltpu.make_async_copy(w_ref, wbuf.at[dp], own_sem)
    own_copy.start()

    acc[...] = jnp.zeros_like(acc)
    own_copy.wait()

    def norm_image(i):
        gain = gain_ref[...]
        fetch = pltpu.make_async_copy(x_ref.at[i], stage, stage_sem)
        fetch.start()
        fetch.wait()

        def norm_rows(r, carry):
            block = layer_norm(stage[pl.ds(pl.multiple_of(r * 16, 16), 16), :], gain, 0.0)
            normed[pl.ds(pl.multiple_of(i * pad + r * 16, 16), 16), :] = block.astype(jnp.bfloat16)
            return carry

        whole = tokens // 16
        lax.fori_loop(0, whole, norm_rows, 0)
        rest = tokens - whole * 16
        if rest:
            last = layer_norm(stage[whole * 16 : tokens, :], gain, 0.0)
            normed[pl.ds(pl.multiple_of(i * pad + whole * 16, 16), 16), :] = jnp.concatenate(
                [last, jnp.zeros((16 - rest, last.shape[1]), jnp.float32)], axis=0
            ).astype(jnp.bfloat16)

    def copy_z(k, s):
        to = lax.rem(t + s, n_tensor)
        return pltpu.make_async_remote_copy(
            src_ref=made.at[k, to // per_image],
            dst_ref=landed.at[s - 1, k],
            send_sem=sz.at[k, s - 1],
            recv_sem=rz.at[k, s - 1],
            device_id={"tensor": to},
            device_id_type=MESH,
        )

    def project(k):
        keys = jnp.zeros((images * pad, HD_T), jnp.float32)
        query = jnp.zeros((images * QROWS, HD_T), jnp.float32)
        for d in range(n_dp):
            deep = slice(d * rows, (d + 1) * rows)
            keys += jnp.dot(
                normed[:, deep], wbuf[d, 1, :, cols(k)], preferred_element_type=jnp.float32
            )
            front = jnp.concatenate(
                [normed[i * pad : i * pad + QROWS, deep] for i in range(images)], axis=0
            )
            query += jnp.dot(front, wbuf[d, 0, :, cols(k)], preferred_element_type=jnp.float32)
        query = (query * HD_T ** (-0.5)).astype(jnp.bfloat16)
        keys = keys.astype(jnp.bfloat16)
        for i in range(images):
            made[k, i, :pad] = keys[i * pad : (i + 1) * pad]
            made[k, i, pad:] = query[i * QROWS : (i + 1) * QROWS]
        for s in range(1, n_tensor):
            copy_z(k, s).start()

    def attend(k):
        for s in range(n_tensor):
            if s:
                copy_z(k, s).wait_recv()
                keys, query = landed[s - 1, k, :pad], landed[s - 1, k, pad:]
            else:
                keys, query = made[k, my_image, :pad], made[k, my_image, pad:]
            scores = lax.dot_general(
                keys, query, (((1,), (1,)), ((), ())), preferred_element_type=jnp.float32
            )
            spot = lax.broadcasted_iota(jnp.int32, scores.shape, 0)
            scores = jnp.where(spot < tokens, scores, -jnp.inf)
            power = jnp.exp(scores - jnp.max(scores, axis=0, keepdims=True))
            maps = power / jnp.sum(power, axis=0, keepdims=True)
            maps = maps.astype(jnp.bfloat16).astype(jnp.float32)
            head = lax.rem(t + n_tensor - s, n_tensor) * heads_here + k
            for h in range(s_part):
                count = counts_ref[head, my_part * s_part + h].astype(jnp.float32)
                acc[s, h] += count * maps

    def step(k, carry):
        @pl.when(k < heads_here)
        def _():
            for s in range(1, n_x):
                copy_x(k, s).wait_recv()
                for g in range(1, n_group):
                    copy_y(k, s, g).start()
                copy_mate_x(k, s).start()

        @pl.when(k > 0)
        def _():
            j = k - 1
            for s in range(1, n_x):
                for g in range(1, n_group):
                    copy_y(j, s, g).wait_recv()
                    copy_mate_y(j, s, g).start()

        @pl.when(k < images)
        def _():
            norm_image(k)

        def ready(j, inner):
            copy_own(j).wait_recv()
            for s in range(1, n_x):
                copy_mate_x(j, s).wait_recv()
                for g in range(1, n_group):
                    copy_mate_y(j, s, g).wait_recv()
            project(j)

            @pl.when(j > 0)
            def _():
                attend(j - 1)

            return inner

        lax.fori_loop(
            jnp.where(k <= images, 0, k - 1), jnp.where(k < images, 0, k), ready, 0
        )
        return carry

    lax.fori_loop(0, heads_here + 1, step, 0)

    attend(heads_here - 1)

    def copy_fold(w, h):
        return pltpu.make_async_remote_copy(
            src_ref=fold.at[w * s_here + h],
            dst_ref=gathered.at[h, dp * images + my_image],
            send_sem=sf.at[w, h],
            recv_sem=rf.at[my_image, h],
            device_id={"tensor": my_part * images + w},
            device_id_type=MESH,
        )

    def arrived_fold(i, h):
        return pltpu.make_async_remote_copy(
            src_ref=fold.at[h],
            dst_ref=gathered.at[h, dp * images + i],
            send_sem=sf.at[0, h],
            recv_sem=rf.at[i, h],
            device_id={"tensor": i * per_image + t // images},
            device_id_type=MESH,
        )

    def copy_dp(s, h):
        own = gathered.at[h, pl.ds(dp * images, images)]
        return pltpu.make_async_remote_copy(
            src_ref=own,
            dst_ref=own,
            send_sem=sg.at[s - 1, h],
            recv_sem=rg.at[s - 1, h],
            device_id={"dp": x_peer(s)},
            device_id_type=MESH,
        )

    def copy_mate(s, h):
        block = gathered.at[h, pl.ds(x_source(s) * images, images)]
        return pltpu.make_async_remote_copy(
            src_ref=block,
            dst_ref=block,
            send_sem=sm.at[s, h],
            recv_sem=rm.at[s, h],
            device_id={"dp": mate},
            device_id_type=MESH,
        )

    for h in range(s_here):
        for w in range(images):
            spot = w * s_here + h
            total = jnp.zeros((pad, QROWS), jnp.float32)
            for s in range(n_tensor):
                total += (acc[s, spot] / DIVISOR).astype(jnp.bfloat16).astype(jnp.float32)
            total = total.astype(jnp.bfloat16)
            fold[spot] = total

            @pl.when(my_part * images + w != t)
            def _():
                copy_fold(w, h).start()

            @pl.when(my_part * images + w == t)
            def _():
                gathered[h, dp * images + my_image] = total

    for h in range(s_here):
        for i in range(images):

            @pl.when(i * per_image + t // images != t)
            def _():
                arrived_fold(i, h).wait_recv()

        for s in range(1, n_x):
            copy_dp(s, h).start()
        copy_mate(0, h).start()
    for h in range(s_here):
        for s in range(1, n_x):
            copy_dp(s, h).wait_recv()
            copy_mate(s, h).start()

    def drain(k, carry):
        for s in range(1, n_x):
            copy_x(k, s).wait_send()
            copy_mate_x(k, s).wait_send()
            for g in range(1, n_group):
                copy_y(k, s, g).wait_send()
                copy_mate_y(k, s, g).wait_send()
        copy_own(k).wait_send()
        for s in range(1, n_tensor):
            copy_z(k, s).wait_send()
        return carry

    lax.fori_loop(0, heads_here, drain, 0)
    for h in range(s_here):
        for w in range(images):

            @pl.when(my_part * images + w != t)
            def _():
                copy_fold(w, h).wait_send()

        for s in range(1, n_x):
            copy_dp(s, h).wait_send()
        for s in range(n_x):
            copy_mate(s, h).wait()
    for h in range(s_here):
        for j in range(images):
            out_ref[h, j] = gathered[h, slots_ref[j]]


def teacher_folded(mesh_sizes, teacher_input, teacher_gain, teacher_weight, head_counts, assignment):
    n_dp, n_group, n_tensor = mesh_sizes
    images, tokens, width = teacher_input.shape
    rows, _, width_here = teacher_weight.shape
    heads_here = width_here // HD_T
    s_heads = head_counts.shape[1]
    s_here = s_heads // n_tensor
    pad = rounded_up(tokens, 16)
    n_x = n_dp // CORES
    s_part = s_heads * images // n_tensor
    split = jnp.transpose(teacher_weight, (1, 0, 2))
    sizes = (n_dp, n_group, n_tensor, heads_here, s_heads, images, tokens)
    dma = pltpu.SemaphoreType.DMA
    one = (heads_here, max(n_x - 1, 1))
    two = one + (max(n_group - 1, 1),)
    return pl.pallas_call(
        functools.partial(teacher_kernel, sizes),
        out_shape=jax.ShapeDtypeStruct((s_here, images, pad, QROWS), jnp.bfloat16),
        in_specs=[
            pl.BlockSpec(memory_space=pltpu.SMEM),
            pl.BlockSpec(memory_space=pltpu.SMEM),
            pl.BlockSpec(memory_space=pl.ANY),
            pl.BlockSpec(memory_space=pltpu.VMEM),
            pl.BlockSpec(memory_space=pl.ANY),
        ],
        out_specs=pl.BlockSpec(memory_space=pltpu.VMEM),
        scratch_shapes=[
            pltpu.VMEM((n_dp, 2, rows, width_here), jnp.bfloat16),
            pltpu.VMEM((images * pad, width), jnp.bfloat16),
            pltpu.VMEM((tokens, width), jnp.bfloat16),
            pltpu.VMEM((n_tensor, s_part, pad, QROWS), jnp.float32),
            pltpu.VMEM((heads_here, images, pad + QROWS, HD_T), jnp.bfloat16),
            pltpu.VMEM((n_tensor - 1, heads_here, pad + QROWS, HD_T), jnp.bfloat16),
            pltpu.VMEM((s_part, pad, QROWS), jnp.bfloat16),
            pltpu.VMEM((s_here, n_dp * images, pad, QROWS), jnp.bfloat16),
            dma,
            dma,
            dma(one),
            dma(one),
            dma(two),
            dma(two),
            dma((heads_here,)),
            dma((heads_here,)),
            dma(one),
            dma(one),
            dma(two),
            dma(two),
            dma((heads_here, n_tensor - 1)),
            dma((heads_here, n_tensor - 1)),
            dma((images, s_here)),
            dma((images, s_here)),
            dma((max(n_x - 1, 1), s_here)),
            dma((max(n_x - 1, 1), s_here)),
            dma((n_x, s_here)),
            dma((n_x, s_here)),
        ],
        compiler_params=pltpu.CompilerParams(
            collective_id=0, has_side_effects=True, vmem_limit_bytes=67043328
        ),
    )(head_counts, assignment, teacher_input, teacher_gain.reshape(1, width), split)


def sum_over_dp(local, n_dp):
    half = local.shape[0] // CORES
    core = lax.rem(lax.axis_index("dp"), CORES)
    mates = [(d, d ^ 1) for d in range(n_dp)]
    rounded = local.astype(jnp.bfloat16)
    mine = lax.dynamic_slice_in_dim(local, core * half, half, 0)
    other = lax.dynamic_slice_in_dim(rounded, (1 - core) * half, half, 0)
    mine = mine + lax.ppermute(other, "dp", mates).astype(jnp.float32)
    sent = mine.astype(jnp.bfloat16)
    for s in range(1, n_dp // CORES):
        around = [(d, (d + CORES * s) % n_dp) for d in range(n_dp)]
        mine = mine + lax.ppermute(sent, "dp", around).astype(jnp.float32)
    done = mine.astype(jnp.bfloat16)
    theirs = lax.ppermute(done, "dp", mates)
    first = jnp.where(core == 0, done, theirs)
    second = jnp.where(core == 0, theirs, done)
    return jnp.concatenate([first, second], axis=0).astype(jnp.float32)


def on_device(
    mesh_sizes,
    teacher_input,
    teacher_gain,
    teacher_weight,
    head_counts,
    assignment,
    student_input,
    student_gain,
    student_bias,
    student_weight,
):
    images, tokens, width_s = student_input.shape
    student_heads = student_weight.shape[1] // (2 * HD_S)
    target = teacher_folded(
        mesh_sizes, teacher_input, teacher_gain, teacher_weight, head_counts, assignment
    )
    target_wide = target.astype(jnp.float32)[:, :, :tokens]
    student_normed = layer_norm(student_input, student_gain, student_bias).astype(jnp.bfloat16)
    normed_front = student_normed[:, :QROWS]
    packed = student_weight.reshape(width_s, student_heads, 2, HD_S)
    weight_query = packed[:, :, 0, :].reshape(width_s, student_heads * HD_S)
    weight_key = packed[:, :, 1, :].reshape(width_s, student_heads * HD_S)
    student_query = (
        jnp.einsum("btd,dc->btc", normed_front, weight_query, preferred_element_type=jnp.float32)
        * HD_S ** (-0.5)
    ).astype(jnp.bfloat16)
    student_keys = jnp.einsum(
        "btd,dc->btc", student_normed, weight_key, preferred_element_type=jnp.float32
    ).astype(jnp.bfloat16)
    split_query = student_query.reshape(images, QROWS, student_heads, HD_S)
    split_keys = student_keys.reshape(images, tokens, student_heads, HD_S)
    probs = jax.nn.softmax(
        jnp.einsum("bqhd,bkhd->hbkq", split_query, split_keys, preferred_element_type=jnp.float32),
        axis=2,
    )
    score_grad = (probs * jnp.sum(target_wide, axis=2, keepdims=True) - target_wide).astype(
        jnp.bfloat16
    )
    query_grad = (
        jnp.einsum("hbkq,bkhd->bqhd", score_grad, split_keys, preferred_element_type=jnp.float32)
        * HD_S ** (-0.5)
    ).astype(jnp.bfloat16)
    key_grad = jnp.einsum(
        "hbkq,bqhd->bkhd", score_grad, split_query, preferred_element_type=jnp.float32
    ).astype(jnp.bfloat16)
    grad_query = jnp.einsum(
        "fkm,fkp->mp",
        normed_front,
        query_grad.reshape(images, QROWS, student_heads * HD_S),
        preferred_element_type=jnp.float32,
    )
    grad_key = jnp.einsum(
        "oip,ois->ps",
        student_normed,
        key_grad.reshape(images, tokens, student_heads * HD_S),
        preferred_element_type=jnp.float32,
    )
    local_grad = jnp.stack(
        [
            grad_query.reshape(width_s, student_heads, HD_S),
            grad_key.reshape(width_s, student_heads, HD_S),
        ],
        axis=2,
    )
    local_grad = local_grad.reshape(width_s, student_heads * 2 * HD_S)
    return sum_over_dp(local_grad, mesh_sizes[0])


def solution(mesh):
    placed = (
        P(("group", "dp"), None, None),
        P(),
        P("dp", None, "tensor"),
        P(),
        P(("group", "dp")),
        P(("group", "dp"), None, None),
        P(),
        P(),
        P(None, "tensor"),
    )
    mesh_sizes = (mesh.shape["dp"], mesh.shape["group"], mesh.shape["tensor"])
    return jax.shard_map(
        functools.partial(on_device, mesh_sizes),
        mesh=mesh,
        in_specs=placed,
        out_specs=P("group", "tensor"),
        check_vma=False,
    )
```

```python
import functools

import jax
import jax.numpy as jnp
from jax import lax
from jax.experimental import pallas as pl
from jax.experimental.pallas import tpu as pltpu
from jax.sharding import PartitionSpec as P

HD_T = 128
HD_S = 64
QROWS = 128
DIVISOR = 72
CORES = 2
MESH = pl.DeviceIdType.MESH


def layer_norm(values, gain, shift):
    wide = values.astype(jnp.float32)
    center = wide - jnp.mean(wide, axis=-1, keepdims=True)
    spread = jnp.mean(center * center, axis=-1, keepdims=True)
    return center * lax.rsqrt(spread + 1e-06) * gain + shift


def rounded_up(value, unit):
    return -(-value // unit) * unit


def teacher_kernel(
    sizes,
    counts_ref,
    slots_ref,
    x_ref,
    gain_ref,
    w_ref,
    out_ref,
    wbuf,
    normed,
    stage,
    acc,
    made,
    landed,
    fold,
    gathered,
    stage_sem,
    own_sem,
    sx,
    rx,
    sy,
    ry,
    so,
    ro,
    spx,
    rpx,
    spy,
    rpy,
    sz,
    rz,
    sf,
    rf,
    sg,
    rg,
    sm,
    rm,
):
    n_dp, n_group, n_tensor, heads_here, s_heads, images, tokens = sizes
    n_x = n_dp // CORES
    rows = w_ref.shape[1]
    rows_part = rows // n_group
    pad = normed.shape[0] // images
    s_here = s_heads // n_tensor
    per_image = n_tensor // images
    s_part = s_heads // per_image

    dp = lax.axis_index("dp")
    y = lax.axis_index("group")
    t = lax.axis_index("tensor")
    x = dp // CORES
    core = lax.rem(dp, CORES)
    mate = x * CORES + (1 - core)
    my_image = t // per_image
    my_part = lax.rem(t, per_image)

    def x_peer(s):
        return lax.rem(x + s, n_x) * CORES + core

    def x_source(s):
        return lax.rem(x + n_x - s, n_x) * CORES + core

    barrier = pltpu.get_barrier_semaphore()
    waits = 0
    for s in range(1, n_dp):
        pl.semaphore_signal(
            barrier, inc=1, device_id={"dp": lax.rem(dp + s, n_dp)}, device_id_type=MESH
        )
        waits += 1
    for s in range(1, n_group):
        pl.semaphore_signal(
            barrier, inc=1, device_id={"group": lax.rem(y + s, n_group)}, device_id_type=MESH
        )
        waits += 1
    for s in range(1, n_tensor):
        pl.semaphore_signal(
            barrier, inc=1, device_id={"tensor": lax.rem(t + s, n_tensor)}, device_id_type=MESH
        )
        waits += 1
    pl.semaphore_wait(barrier, waits)

    def cols(k):
        return pl.ds(pl.multiple_of(k * HD_T, HD_T), HD_T)

    def band(g):
        return pl.ds(pl.multiple_of(g * rows_part, 16), rows_part)

    def copy_x(k, s):
        return pltpu.make_async_remote_copy(
            src_ref=w_ref.at[:, band(y), cols(k)],
            dst_ref=wbuf.at[dp, :, band(y), cols(k)],
            send_sem=sx.at[k, s - 1],
            recv_sem=rx.at[k, s - 1],
            device_id={"dp": x_peer(s)},
            device_id_type=MESH,
        )

    def copy_own(k):
        return pltpu.make_async_remote_copy(
            src_ref=w_ref.at[:, :, cols(k)],
            dst_ref=wbuf.at[dp, :, :, cols(k)],
            send_sem=so.at[k],
            recv_sem=ro.at[k],
            device_id={"dp": mate},
            device_id_type=MESH,
        )

    def copy_y(k, s, g):
        where = (x_source(s), slice(None), band(y), cols(k))
        return pltpu.make_async_remote_copy(
            src_ref=wbuf.at[where],
            dst_ref=wbuf.at[where],
            send_sem=sy.at[k, s - 1, g - 1],
            recv_sem=ry.at[k, s - 1, g - 1],
            device_id={"group": lax.rem(y + g, n_group)},
            device_id_type=MESH,
        )

    def copy_mate_x(k, s):
        where = (x_source(s), slice(None), band(y), cols(k))
        return pltpu.make_async_remote_copy(
            src_ref=wbuf.at[where],
            dst_ref=wbuf.at[where],
            send_sem=spx.at[k, s - 1],
            recv_sem=rpx.at[k, s - 1],
            device_id={"dp": mate},
            device_id_type=MESH,
        )

    def copy_mate_y(k, s, g):
        where = (x_source(s), slice(None), band(lax.rem(y + n_group - g, n_group)), cols(k))
        return pltpu.make_async_remote_copy(
            src_ref=wbuf.at[where],
            dst_ref=wbuf.at[where],
            send_sem=spy.at[k, s - 1, g - 1],
            recv_sem=rpy.at[k, s - 1, g - 1],
            device_id={"dp": mate},
            device_id_type=MESH,
        )

    def open_sends(k, carry):
        for s in range(1, n_x):
            copy_x(k, s).start()
        copy_own(k).start()
        return carry

    lax.fori_loop(0, heads_here, open_sends, 0)
    own_copy = pltpu.make_async_copy(w_ref, wbuf.at[dp], own_sem)
    own_copy.start()

    acc[...] = jnp.zeros_like(acc)
    own_copy.wait()

    def norm_image(i):
        gain = gain_ref[...]
        fetch = pltpu.make_async_copy(x_ref.at[i], stage, stage_sem)
        fetch.start()
        fetch.wait()

        def norm_rows(r, carry):
            block = layer_norm(stage[pl.ds(pl.multiple_of(r * 16, 16), 16), :], gain, 0.0)
            normed[pl.ds(pl.multiple_of(i * pad + r * 16, 16), 16), :] = block.astype(jnp.bfloat16)
            return carry

        whole = tokens // 16
        lax.fori_loop(0, whole, norm_rows, 0)
        rest = tokens - whole * 16
        if rest:
            last = layer_norm(stage[whole * 16 : tokens, :], gain, 0.0)
            normed[pl.ds(pl.multiple_of(i * pad + whole * 16, 16), 16), :] = jnp.concatenate(
                [last, jnp.zeros((16 - rest, last.shape[1]), jnp.float32)], axis=0
            ).astype(jnp.bfloat16)

    def copy_z(k, s):
        to = lax.rem(t + s, n_tensor)
        return pltpu.make_async_remote_copy(
            src_ref=made.at[k, to // per_image],
            dst_ref=landed.at[s - 1, k],
            send_sem=sz.at[k, s - 1],
            recv_sem=rz.at[k, s - 1],
            device_id={"tensor": to},
            device_id_type=MESH,
        )

    def project(k):
        keys = jnp.zeros((images * pad, HD_T), jnp.float32)
        query = jnp.zeros((images * QROWS, HD_T), jnp.float32)
        for d in range(n_dp):
            deep = slice(d * rows, (d + 1) * rows)
            keys += jnp.dot(
                normed[:, deep], wbuf[d, 1, :, cols(k)], preferred_element_type=jnp.float32
            )
            front = jnp.concatenate(
                [normed[i * pad : i * pad + QROWS, deep] for i in range(images)], axis=0
            )
            query += jnp.dot(front, wbuf[d, 0, :, cols(k)], preferred_element_type=jnp.float32)
        query = (query * HD_T ** (-0.5)).astype(jnp.bfloat16)
        keys = keys.astype(jnp.bfloat16)
        for i in range(images):
            made[k, i, :pad] = keys[i * pad : (i + 1) * pad]
            made[k, i, pad:] = query[i * QROWS : (i + 1) * QROWS]
        for s in range(1, n_tensor):
            copy_z(k, s).start()

    def attend(k):
        for s in range(n_tensor):
            if s:
                copy_z(k, s).wait_recv()
                keys, query = landed[s - 1, k, :pad], landed[s - 1, k, pad:]
            else:
                keys, query = made[k, my_image, :pad], made[k, my_image, pad:]
            scores = lax.dot_general(
                keys, query, (((1,), (1,)), ((), ())), preferred_element_type=jnp.float32
            )
            spot = lax.broadcasted_iota(jnp.int32, scores.shape, 0)
            scores = jnp.where(spot < tokens, scores, -jnp.inf)
            power = jnp.exp(scores - jnp.max(scores, axis=0, keepdims=True))
            maps = power / jnp.sum(power, axis=0, keepdims=True)
            maps = maps.astype(jnp.bfloat16).astype(jnp.float32)
            head = lax.rem(t + n_tensor - s, n_tensor) * heads_here + k
            for h in range(s_part):
                count = counts_ref[head, my_part * s_part + h].astype(jnp.float32)
                acc[s, h] += count * maps

    def step(k, carry):
        @pl.when(k < heads_here)
        def _():
            for s in range(1, n_x):
                copy_x(k, s).wait_recv()
                for g in range(1, n_group):
                    copy_y(k, s, g).start()
                copy_mate_x(k, s).start()

        @pl.when((k > 0) & (k <= heads_here))
        def _():
            j = k - 1
            for s in range(1, n_x):
                for g in range(1, n_group):
                    copy_y(j, s, g).wait_recv()
                    copy_mate_y(j, s, g).start()

        @pl.when(k < images)
        def _():
            norm_image(k)

        def ready(j, inner):
            copy_own(j).wait_recv()
            for s in range(1, n_x):
                copy_mate_x(j, s).wait_recv()
                for g in range(1, n_group):
                    copy_mate_y(j, s, g).wait_recv()
            project(j)

            @pl.when(j > 0)
            def _():
                attend(j - 1)

            return inner

        lax.fori_loop(
            jnp.where(k <= images, 0, k - 2), jnp.where(k < images, 0, k - 1), ready, 0
        )
        return carry

    lax.fori_loop(0, heads_here + 2, step, 0)

    attend(heads_here - 1)

    def copy_fold(w, h):
        return pltpu.make_async_remote_copy(
            src_ref=fold.at[w * s_here + h],
            dst_ref=gathered.at[h, dp * images + my_image],
            send_sem=sf.at[w, h],
            recv_sem=rf.at[my_image, h],
            device_id={"tensor": my_part * images + w},
            device_id_type=MESH,
        )

    def arrived_fold(i, h):
        return pltpu.make_async_remote_copy(
            src_ref=fold.at[h],
            dst_ref=gathered.at[h, dp * images + i],
            send_sem=sf.at[0, h],
            recv_sem=rf.at[i, h],
            device_id={"tensor": i * per_image + t // images},
            device_id_type=MESH,
        )

    def copy_dp(s, h):
        own = gathered.at[h, pl.ds(dp * images, images)]
        return pltpu.make_async_remote_copy(
            src_ref=own,
            dst_ref=own,
            send_sem=sg.at[s - 1, h],
            recv_sem=rg.at[s - 1, h],
            device_id={"dp": x_peer(s)},
            device_id_type=MESH,
        )

    def copy_mate(s, h):
        block = gathered.at[h, pl.ds(x_source(s) * images, images)]
        return pltpu.make_async_remote_copy(
            src_ref=block,
            dst_ref=block,
            send_sem=sm.at[s, h],
            recv_sem=rm.at[s, h],
            device_id={"dp": mate},
            device_id_type=MESH,
        )

    for h in range(s_here):
        for w in range(images):
            spot = w * s_here + h
            total = jnp.zeros((pad, QROWS), jnp.float32)
            for s in range(n_tensor):
                total += (acc[s, spot] / DIVISOR).astype(jnp.bfloat16).astype(jnp.float32)
            total = total.astype(jnp.bfloat16)
            fold[spot] = total

            @pl.when(my_part * images + w != t)
            def _():
                copy_fold(w, h).start()

            @pl.when(my_part * images + w == t)
            def _():
                gathered[h, dp * images + my_image] = total

    for h in range(s_here):
        for i in range(images):

            @pl.when(i * per_image + t // images != t)
            def _():
                arrived_fold(i, h).wait_recv()

        for s in range(1, n_x):
            copy_dp(s, h).start()
        copy_mate(0, h).start()
    for h in range(s_here):
        for s in range(1, n_x):
            copy_dp(s, h).wait_recv()
            copy_mate(s, h).start()

    def drain(k, carry):
        for s in range(1, n_x):
            copy_x(k, s).wait_send()
            copy_mate_x(k, s).wait_send()
            for g in range(1, n_group):
                copy_y(k, s, g).wait_send()
                copy_mate_y(k, s, g).wait_send()
        copy_own(k).wait_send()
        for s in range(1, n_tensor):
            copy_z(k, s).wait_send()
        return carry

    lax.fori_loop(0, heads_here, drain, 0)
    for h in range(s_here):
        for w in range(images):

            @pl.when(my_part * images + w != t)
            def _():
                copy_fold(w, h).wait_send()

        for s in range(1, n_x):
            copy_dp(s, h).wait_send()
        for s in range(n_x):
            copy_mate(s, h).wait()
    for h in range(s_here):
        for j in range(images):
            out_ref[h, j] = gathered[h, slots_ref[j]]


def teacher_folded(mesh_sizes, teacher_input, teacher_gain, teacher_weight, head_counts, assignment):
    n_dp, n_group, n_tensor = mesh_sizes
    images, tokens, width = teacher_input.shape
    rows, _, width_here = teacher_weight.shape
    heads_here = width_here // HD_T
    s_heads = head_counts.shape[1]
    s_here = s_heads // n_tensor
    pad = rounded_up(tokens, 16)
    n_x = n_dp // CORES
    s_part = s_heads * images // n_tensor
    split = jnp.transpose(teacher_weight, (1, 0, 2))
    sizes = (n_dp, n_group, n_tensor, heads_here, s_heads, images, tokens)
    dma = pltpu.SemaphoreType.DMA
    one = (heads_here, max(n_x - 1, 1))
    two = one + (max(n_group - 1, 1),)
    return pl.pallas_call(
        functools.partial(teacher_kernel, sizes),
        out_shape=jax.ShapeDtypeStruct((s_here, images, pad, QROWS), jnp.bfloat16),
        in_specs=[
            pl.BlockSpec(memory_space=pltpu.SMEM),
            pl.BlockSpec(memory_space=pltpu.SMEM),
            pl.BlockSpec(memory_space=pl.ANY),
            pl.BlockSpec(memory_space=pltpu.VMEM),
            pl.BlockSpec(memory_space=pl.ANY),
        ],
        out_specs=pl.BlockSpec(memory_space=pltpu.VMEM),
        scratch_shapes=[
            pltpu.VMEM((n_dp, 2, rows, width_here), jnp.bfloat16),
            pltpu.VMEM((images * pad, width), jnp.bfloat16),
            pltpu.VMEM((tokens, width), jnp.bfloat16),
            pltpu.VMEM((n_tensor, s_part, pad, QROWS), jnp.float32),
            pltpu.VMEM((heads_here, images, pad + QROWS, HD_T), jnp.bfloat16),
            pltpu.VMEM((n_tensor - 1, heads_here, pad + QROWS, HD_T), jnp.bfloat16),
            pltpu.VMEM((s_part, pad, QROWS), jnp.bfloat16),
            pltpu.VMEM((s_here, n_dp * images, pad, QROWS), jnp.bfloat16),
            dma,
            dma,
            dma(one),
            dma(one),
            dma(two),
            dma(two),
            dma((heads_here,)),
            dma((heads_here,)),
            dma(one),
            dma(one),
            dma(two),
            dma(two),
            dma((heads_here, n_tensor - 1)),
            dma((heads_here, n_tensor - 1)),
            dma((images, s_here)),
            dma((images, s_here)),
            dma((max(n_x - 1, 1), s_here)),
            dma((max(n_x - 1, 1), s_here)),
            dma((n_x, s_here)),
            dma((n_x, s_here)),
        ],
        compiler_params=pltpu.CompilerParams(
            collective_id=0, has_side_effects=True, vmem_limit_bytes=67043328
        ),
    )(head_counts, assignment, teacher_input, teacher_gain.reshape(1, width), split)


def sum_over_dp(local, n_dp):
    half = local.shape[0] // CORES
    core = lax.rem(lax.axis_index("dp"), CORES)
    mates = [(d, d ^ 1) for d in range(n_dp)]
    rounded = local.astype(jnp.bfloat16)
    mine = lax.dynamic_slice_in_dim(local, core * half, half, 0)
    other = lax.dynamic_slice_in_dim(rounded, (1 - core) * half, half, 0)
    mine = mine + lax.ppermute(other, "dp", mates).astype(jnp.float32)
    sent = mine.astype(jnp.bfloat16)
    for s in range(1, n_dp // CORES):
        around = [(d, (d + CORES * s) % n_dp) for d in range(n_dp)]
        mine = mine + lax.ppermute(sent, "dp", around).astype(jnp.float32)
    done = mine.astype(jnp.bfloat16)
    theirs = lax.ppermute(done, "dp", mates)
    first = jnp.where(core == 0, done, theirs)
    second = jnp.where(core == 0, theirs, done)
    return jnp.concatenate([first, second], axis=0).astype(jnp.float32)


def on_device(
    mesh_sizes,
    teacher_input,
    teacher_gain,
    teacher_weight,
    head_counts,
    assignment,
    student_input,
    student_gain,
    student_bias,
    student_weight,
):
    images, tokens, width_s = student_input.shape
    student_heads = student_weight.shape[1] // (2 * HD_S)
    target = teacher_folded(
        mesh_sizes, teacher_input, teacher_gain, teacher_weight, head_counts, assignment
    )
    target_wide = target.astype(jnp.float32)[:, :, :tokens]
    student_normed = layer_norm(student_input, student_gain, student_bias).astype(jnp.bfloat16)
    normed_front = student_normed[:, :QROWS]
    packed = student_weight.reshape(width_s, student_heads, 2, HD_S)
    weight_query = packed[:, :, 0, :].reshape(width_s, student_heads * HD_S)
    weight_key = packed[:, :, 1, :].reshape(width_s, student_heads * HD_S)
    student_query = (
        jnp.einsum("btd,dc->btc", normed_front, weight_query, preferred_element_type=jnp.float32)
        * HD_S ** (-0.5)
    ).astype(jnp.bfloat16)
    student_keys = jnp.einsum(
        "btd,dc->btc", student_normed, weight_key, preferred_element_type=jnp.float32
    ).astype(jnp.bfloat16)
    split_query = student_query.reshape(images, QROWS, student_heads, HD_S)
    split_keys = student_keys.reshape(images, tokens, student_heads, HD_S)
    probs = jax.nn.softmax(
        jnp.einsum("bqhd,bkhd->hbkq", split_query, split_keys, preferred_element_type=jnp.float32),
        axis=2,
    )
    score_grad = (probs * jnp.sum(target_wide, axis=2, keepdims=True) - target_wide).astype(
        jnp.bfloat16
    )
    query_grad = (
        jnp.einsum("hbkq,bkhd->bqhd", score_grad, split_keys, preferred_element_type=jnp.float32)
        * HD_S ** (-0.5)
    ).astype(jnp.bfloat16)
    key_grad = jnp.einsum(
        "hbkq,bqhd->bkhd", score_grad, split_query, preferred_element_type=jnp.float32
    ).astype(jnp.bfloat16)
    grad_query = jnp.einsum(
        "fkm,fkp->mp",
        normed_front,
        query_grad.reshape(images, QROWS, student_heads * HD_S),
        preferred_element_type=jnp.float32,
    )
    grad_key = jnp.einsum(
        "oip,ois->ps",
        student_normed,
        key_grad.reshape(images, tokens, student_heads * HD_S),
        preferred_element_type=jnp.float32,
    )
    local_grad = jnp.stack(
        [
            grad_query.reshape(width_s, student_heads, HD_S),
            grad_key.reshape(width_s, student_heads, HD_S),
        ],
        axis=2,
    )
    local_grad = local_grad.reshape(width_s, student_heads * 2 * HD_S)
    return sum_over_dp(local_grad, mesh_sizes[0])


def solution(mesh):
    placed = (
        P(("group", "dp"), None, None),
        P(),
        P("dp", None, "tensor"),
        P(),
        P(("group", "dp")),
        P(("group", "dp"), None, None),
        P(),
        P(),
        P(None, "tensor"),
    )
    mesh_sizes = (mesh.shape["dp"], mesh.shape["group"], mesh.shape["tensor"])
    return jax.shard_map(
        functools.partial(on_device, mesh_sizes),
        mesh=mesh,
        in_specs=placed,
        out_specs=P("group", "tensor"),
        check_vma=False,
    )
```
